256 devices in a mesh: panel: 4 (over x), front: 64 (over y, z, core).
Axes of the slice: x: 4, y: 4, z: 8, core: 2. Of those that a mesh axis runs over, the one named last changes fastest.
Arguments:
- top_source: bfloat16 [4, 128, 4096], P('panel', None, 'front'), may hold values from -6 to 6
- leaf_source: bfloat16 [4, 128, 589824], P('panel', None, 'front'), may hold values from -6 to 6
- top_inverse: bfloat16 [4, 4096, 4096], P('panel', 'front'), may hold values from -1 to 4
- leaf_inverse: bfloat16 [4, 2304, 256, 256], P('panel', 'front'), may hold values from -1 to 4
- boundary: bfloat16 [4, 2304, 128, 256], P('panel', 'front'), may hold values from -0.09375 to 0.09375
- touch_rows: int32 [4, 2304, 128], P('panel', 'front'), may hold values from 0 to 4095, as said below
- coupling: float32 [4, 4096], P('panel', 'front'), may hold values from 0.3 to 1
Outputs:
- top_field: bfloat16 [4, 128, 4096], P('panel', None, 'front')
- leaf_field: bfloat16 [4, 128, 589824], P('panel', None, 'front')
The draws below stay inside these ranges and needn't reach their ends.
Inputs may be any that keep to these rules, and one draw needn't show every extreme that they name: `touch_rows`: front index d owns top front rows d * 64 to (d + 1) * 64 - 1; leaf j of a panel touches only rows owned by front indices j // 36 - 1, j // 36 and j // 36 + 1.
All inputs are finite; a program needn't handle non-finite values.
Results may differ from the reference program's by a relative error of at most 0.02.
Values may be sent and summed in bfloat16 or wider, within the bound.
A program may use at most 64 MiB of HBM per device.

```python
import math
import jax
import jax.numpy as jnp
from jax import lax

TOP_WIDTH = 4096
LEAF_WIDTH = 256
EDGE_ROWS = 128
LEAVES = 36
SOURCES = 128
PANELS = 4
LEAVES_ALL = 2304


def dominant(key, blocks, matrix_order):
    diag_key, off_key = jax.random.split(key)
    diagonal = jnp.exp(jax.random.uniform(diag_key, (blocks, matrix_order), jnp.float32, -0.7, 0.7))
    spread = jax.random.truncated_normal(off_key, -4.0, 4.0, (blocks, matrix_order, matrix_order), jnp.float32) * (0.5 / matrix_order ** 0.5)
    same_cell = lax.broadcasted_iota(jnp.int32, (matrix_order, matrix_order), 0) == lax.broadcasted_iota(jnp.int32, (matrix_order, matrix_order), 1)
    return jnp.where(same_cell[None], diagonal[:, :, None], spread)


def draw_top_inverse(key, part):
    folded = jax.random.fold_in(key, 11)
    return dominant(folded, PANELS, TOP_WIDTH).astype(jnp.bfloat16)


def draw_leaf_inverse(key, part):
    folded = jax.random.fold_in(key, 23)
    blocks = dominant(folded, PANELS * LEAVES_ALL, LEAF_WIDTH)
    return blocks.reshape(PANELS, LEAVES_ALL, LEAF_WIDTH, LEAF_WIDTH).astype(jnp.bfloat16)


def draw_touch_rows(key, part):
    folded = jax.random.fold_in(key, 37)
    shard_rows = TOP_WIDTH * LEAVES // LEAVES_ALL
    shape = (PANELS, LEAVES_ALL, EDGE_ROWS)
    leaf_ids = lax.broadcasted_iota(jnp.int32, shape, 1)
    edge_ids = lax.broadcasted_iota(jnp.int32, shape, 2)
    owner = leaf_ids // LEAVES
    centre = owner * shard_rows + leaf_ids % LEAVES * shard_rows // LEAVES
    offsets = jax.random.randint(folded, shape, -shard_rows, shard_rows, dtype=jnp.int32)
    offsets = jnp.where(edge_ids == 0, 0, offsets)
    return jnp.clip(centre + offsets, 0, TOP_WIDTH - 1).astype(jnp.int32)


def shard_levels(key, dims, cuts, low, top_value):
    loudness, own = 1.0, jax.random.fold_in(key, 6)
    for dim, blocks in cuts:
        steps = jnp.exp(jax.random.uniform(jax.random.fold_in(own, dim), (blocks,), jnp.float32, low / len(cuts), top_value / len(cuts)))
        loudness = loudness * jnp.repeat(steps, dims[dim] // blocks).reshape([-1 if axis == dim else 1 for axis in range(len(dims))])
    return loudness


def normal_values(rng, dims, width, reach, pieces=(), kind=jnp.bfloat16):
    entries = width * jax.random.normal(rng, dims, jnp.float32)
    if pieces:
        entries = entries * shard_levels(rng, dims, pieces, -0.22, 0.18)
    return jnp.clip(entries, -reach, reach).astype(kind)


def setup_inputs(seed: int = 0) -> dict:
    key_of = jax.random.split(jax.random.key(seed), 8)
    return {
        "top_source": normal_values(key_of[0], (PANELS, SOURCES, TOP_WIDTH), 1.0, 6.0, ((0, 4), (2, 64))),
        "leaf_source": normal_values(key_of[1], (PANELS, SOURCES, LEAVES_ALL * LEAF_WIDTH), 1.0, 6.0, ((0, 4), (2, 64))),
        "top_inverse": draw_top_inverse(jax.random.fold_in(key_of[7], 71), 0),
        "leaf_inverse": draw_leaf_inverse(jax.random.fold_in(key_of[7], 71), 0),
        "boundary": normal_values(key_of[4], (PANELS, LEAVES_ALL, EDGE_ROWS, LEAF_WIDTH), (16 * LEAF_WIDTH) ** -0.5, 0.09375, ((0, 4), (1, 64))),
        "touch_rows": draw_touch_rows(jax.random.fold_in(key_of[7], 71), 0),
        "coupling": jnp.clip(jnp.exp(math.log(1.0) - 1.2039728 * jax.random.uniform(key_of[6], (PANELS, TOP_WIDTH), jnp.float32) ** shard_levels(key_of[6], (PANELS, TOP_WIDTH), ((0, 4), (1, 64)), -0.2, 0.2)), 0.3, 1.0),
    }


def leaf_apply(inverse_blocks, vectors):
    return jnp.einsum("jab,sjb->sja", inverse_blocks.astype(jnp.float32), vectors.astype(jnp.float32))


def lift_rows(boundary_rows, picked):
    return jnp.einsum("jkb,sjk->sjb", boundary_rows.astype(jnp.float32), picked.astype(jnp.float32))


def reference(top_source, leaf_source, top_inverse, leaf_inverse, boundary, touch_rows, coupling):
    previous = jnp.zeros((SOURCES, TOP_WIDTH), jnp.bfloat16)
    forward_tops = []
    forward_leaves = []
    for panel_index in range(PANELS):
        flat_rows = touch_rows[panel_index].reshape(-1).astype(jnp.int32)
        vectors = leaf_source[panel_index].reshape(SOURCES, LEAVES_ALL, LEAF_WIDTH)
        interior = leaf_apply(leaf_inverse[panel_index], vectors).astype(jnp.bfloat16)
        pushed = jnp.einsum("jkb,sjb->sjk", boundary[panel_index].astype(jnp.float32), interior.astype(jnp.float32))
        gathered = jnp.zeros((SOURCES, TOP_WIDTH), jnp.float32).at[:, flat_rows].add(pushed.reshape(SOURCES, -1))
        rhs_rows = (top_source[panel_index].astype(jnp.float32) + coupling[panel_index] * previous.astype(jnp.float32) - gathered).astype(jnp.bfloat16)
        solved = jnp.dot(rhs_rows, top_inverse[panel_index].T, preferred_element_type=jnp.float32).astype(jnp.bfloat16)
        picked = solved[:, flat_rows].reshape(SOURCES, LEAVES_ALL, EDGE_ROWS)
        lifted = lift_rows(boundary[panel_index], picked).astype(jnp.bfloat16)
        leaf_out = (interior.astype(jnp.float32) - leaf_apply(leaf_inverse[panel_index], lifted)).astype(jnp.bfloat16)
        forward_tops.append(solved)
        forward_leaves.append(leaf_out)
        previous = solved
    arriving = jnp.zeros((SOURCES, TOP_WIDTH), jnp.bfloat16)
    top_final = [None] * PANELS
    leaf_final = [None] * PANELS
    for panel_index in reversed(range(PANELS)):
        flat_rows = touch_rows[panel_index].reshape(-1).astype(jnp.int32)
        correction = jnp.dot(arriving, top_inverse[panel_index].T, preferred_element_type=jnp.float32).astype(jnp.bfloat16)
        top_out = (forward_tops[panel_index].astype(jnp.float32) + correction.astype(jnp.float32)).astype(jnp.bfloat16)
        picked = correction[:, flat_rows].reshape(SOURCES, LEAVES_ALL, EDGE_ROWS)
        raised = lift_rows(boundary[panel_index], picked).astype(jnp.bfloat16)
        leaf_out = (forward_leaves[panel_index].astype(jnp.float32) - leaf_apply(leaf_inverse[panel_index], raised)).astype(jnp.bfloat16)
        top_final[panel_index] = top_out
        leaf_final[panel_index] = leaf_out.reshape(SOURCES, LEAVES_ALL * LEAF_WIDTH)
        arriving = (coupling[panel_index] * top_out.astype(jnp.float32)).astype(jnp.bfloat16)
    return jnp.stack(top_final), jnp.stack(leaf_final)
```

```python
import functools

import jax
import jax.numpy as jnp
from jax import lax
from jax.experimental import pallas as pl
from jax.experimental.pallas import tpu as pltpu
from jax.sharding import PartitionSpec as P

MESH = pl.DeviceIdType.MESH
BF = jnp.bfloat16
F32 = jnp.float32
NT = (((1,), (1,)), ((), ()))
NN = (((1,), (0,)), ((), ()))
STEPS = 7
GROUP = 16


def dot(a, b, dims):
    return lax.dot_general(a, b, dims, preferred_element_type=F32)


def kernel(
    sizes,
    ts_hbm, ls_hbm, ti_hbm, li_hbm, bd_hbm, tr_hbm, cp_hbm,
    tf_hbm, lf_hbm,
    ts, vec, inv, bnd, rows, cpl,
    inner, lift, acc, main, halo, main_in, halo_in, tops, gath, tabs, field, own_w, nb_w, half,
    in_sem, small_sem, out_sem,
    ta_send, ta_recv, tc_send, tc_recv,
    pm_send, pm_recv, ph_send, ph_recv,
    z_send, y_send, g_recv, o_send, o_recv,
):
    ny, nz, chunks, per = sizes
    chips = ny * nz
    panels = 4
    r = lax.axis_index("panel")
    f = lax.axis_index("front")
    m, c = lax.div(f, 2), lax.rem(f, 2)
    y, z = lax.div(m, nz), lax.rem(m, nz)
    other = 1 - c
    up, down = lax.rem(m + 1, chips), lax.rem(m + chips - 1, chips)
    side = lax.rem(m + chips - 1 + 2 * c, chips)

    def dev(q, chip, core):
        return (q, chip * 2 + core)

    def remote(src, dst, send, recv, where):
        return pltpu.make_async_remote_copy(
            src_ref=src, dst_ref=dst, send_sem=send, recv_sem=recv,
            device_id=where, device_id_type=MESH,
        )

    width = ls_hbm.shape[2] // chunks // per

    small = [
        pltpu.make_async_copy(ts_hbm.at[0], ts, small_sem.at[0]),
        pltpu.make_async_copy(tr_hbm.at[0], rows, small_sem.at[1]),
        pltpu.make_async_copy(cp_hbm, cpl, small_sem.at[2]),
        pltpu.make_async_copy(
            ti_hbm.at[0], tops.at[r, pl.ds(pl.multiple_of(c * 64, 64), 64)], small_sem.at[3]
        ),
    ]
    big = []
    for g in range(chunks):
        at = pl.ds(g * per, per)
        cols = pl.ds(g * per * width, per * width)
        big.append((
            pltpu.make_async_copy(bd_hbm.at[0, at], bnd.at[at], in_sem.at[0, g]),
            pltpu.make_async_copy(li_hbm.at[0, at], inv.at[at], in_sem.at[1, g]),
            pltpu.make_async_copy(ls_hbm.at[0, :, cols], vec.at[:, cols], in_sem.at[2, g]),
        ))
    small[1].start()
    for copy in big[0]:
        copy.start()
    for copy in (small[0], small[2], small[3]):
        copy.start()
    for group in big[1:]:
        for copy in group:
            copy.start()

    barrier = pltpu.get_barrier_semaphore()
    count = 0
    for dq in range(panels):
        q = lax.rem(r + dq, panels)
        for core in (c, other):
            for chip in (m, up, down):
                if dq == 0 and core is c and chip is m:
                    continue
                pl.semaphore_signal(barrier, inc=1, device_id=dev(q, chip, core), device_id_type=MESH)
                count += 1
    for dz in range(1, nz):
        peer = dev(r, y * nz + lax.rem(z + dz, nz), c)
        pl.semaphore_signal(barrier, inc=1, device_id=peer, device_id_type=MESH)
        count += 1
    for dy in range(1, ny):
        peer = dev(r, lax.rem(y + dy, ny) * nz + z, c)
        pl.semaphore_signal(barrier, inc=1, device_id=peer, device_id_type=MESH)
        count += 1
    pl.semaphore_wait(barrier, count)

    right, left, far = lax.rem(r + 1, 4), lax.rem(r + 3, 4), lax.rem(r + 2, 4)

    def rows_of(q, core, start=0, size=64):
        return tops.at[q, pl.ds(pl.multiple_of(core * 64 + start, 32), size)]

    sent_a = [
        remote(ti_hbm.at[0], rows_of(r, c), ta_send.at[0], ta_recv.at[0], dev(right, m, c)),
        remote(ti_hbm.at[0], rows_of(r, c), ta_send.at[1], ta_recv.at[1], dev(left, m, c)),
        remote(ti_hbm.at[0], rows_of(r, c), tc_send.at[0], tc_recv.at[0], dev(r, m, other)),
    ]
    for copy in sent_a:
        copy.start()

    acc[...] = jnp.zeros_like(acc)
    base = m * 128
    small[1].wait()

    def leaf(j):
        u = jnp.bitwise_and(rows[pl.ds(j, 1), :] - base, 255)
        hot = lax.broadcasted_iota(jnp.int32, (256, u.shape[1]), 0) == u
        hot = jnp.where(hot, 1.0, 0.0).astype(BF)
        spread = dot(hot, bnd[j], NN).astype(BF)
        cols = pl.ds(pl.multiple_of(j * width, width), width)
        both = dot(jnp.concatenate([vec[:, cols], spread], axis=0), inv[j], NT).astype(BF)
        inner[:, cols] = both[:128]
        lift[:, cols] = both[128:]
        return dot(both[:128], spread, NT)

    for g in range(chunks):
        for copy in big[g]:
            copy.wait()

        def body(i, carry):
            first = g * per + i * 3
            acc[...] += leaf(first) + leaf(first + 1) + leaf(first + 2)
            return carry

        lax.fori_loop(0, per // 3, body, 0)

    for k in (0, 2):
        small[k].wait()
    known = -acc[:, :128]
    local = ts[...].astype(F32)
    zero = jnp.zeros_like(local)
    lower = jnp.where(c == 0, local, zero)
    upper = jnp.where(c == 0, zero, local)
    known = known + jnp.concatenate([lower, upper], axis=1)
    scale = cpl[...]
    blank = jnp.zeros_like(scale)
    scale = jnp.concatenate(
        [jnp.where(c == 0, scale, blank), jnp.where(c == 0, blank, scale)], axis=1
    )
    scale = jnp.broadcast_to(scale, (8, 128))
    for k in range(8):
        main[k, :GROUP] = known[k * GROUP : (k + 1) * GROUP]
        main[k, GROUP:] = scale
        halo[k] = -acc[k * GROUP : (k + 1) * GROUP, 128:]
    mine = r * 2 + c
    main_in[r, c] = main[mine]

    piece_sends = []
    for dq in range(panels):
        q = lax.rem(r + dq, panels)
        for n, core in enumerate((c, other)):
            k, slot = q * 2 + core, dq * 2 + n
            if slot:
                piece_sends.append(remote(
                    main.at[k], main_in.at[r, c], pm_send.at[slot], pm_recv.at[r, c], dev(q, m, core)
                ))
            piece_sends.append(remote(
                halo.at[k], halo_in.at[r, c], ph_send.at[slot], ph_recv.at[r, c], dev(q, side, core)
            ))
    for copy in piece_sends:
        copy.start()

    sent_a[0].wait_recv()
    relays = [
        remote(rows_of(left, c, 0, 32), rows_of(left, c, 0, 32), ta_send.at[2], ta_recv.at[2], dev(right, m, c)),
        remote(rows_of(left, c), rows_of(left, c), tc_send.at[1], tc_recv.at[1], dev(r, m, other)),
    ]
    for copy in relays:
        copy.start()
    sent_a[1].wait_recv()
    more = [
        remote(rows_of(right, c, 32, 32), rows_of(right, c, 32, 32), ta_send.at[3], ta_recv.at[3], dev(left, m, c)),
        remote(rows_of(right, c), rows_of(right, c), tc_send.at[2], tc_recv.at[2], dev(r, m, other)),
    ]
    for copy in more:
        copy.start()
    relays += more

    def finish_tops():
        small[3].wait()
        last = remote(rows_of(far, c), rows_of(far, c), tc_send.at[3], tc_recv.at[3], dev(r, m, other))
        relays[0].wait_recv()
        relays[2].wait_recv()
        last.start()
        for copy in (sent_a[2], relays[1], relays[3], last):
            copy.wait_recv()
        for copy in sent_a + relays + [last]:
            copy.wait_send()

    def meet_pieces(p):
        for core in (0, 1):
            arrival = remote(main.at[0], main_in.at[p, core], pm_send.at[0], pm_recv.at[p, core], dev(r, m, other))

            @pl.when(jnp.logical_or(p != r, c != core))
            def _():
                arrival.wait_recv()

            remote(halo.at[0], halo_in.at[p, core], ph_send.at[0], ph_recv.at[p, core], dev(r, m, other)).wait_recv()
        a, b = main_in[p, 0], main_in[p, 1]
        tabs[p] = a[:GROUP] + b[:GROUP] + halo_in[p, 0] + halo_in[p, 1]
        pair = a[GROUP:] + b[GROUP:]
        tabs[4 + p] = jnp.concatenate([pair, pair], axis=0)

    def z_copy(t, s, dz):
        return remote(
            gath.at[t, m], gath.at[t, m], z_send.at[s, dz - 1], g_recv.at[s, m],
            dev(r, y * nz + lax.rem(z + dz, nz), c),
        )

    def y_copy(t, s, dz, dy):
        tile = y * nz + lax.rem(z + dz, nz)
        return remote(
            gath.at[t, tile], gath.at[t, tile], y_send.at[s, dz, dy - 1], g_recv.at[s, tile],
            dev(r, lax.rem(y + dy, ny) * nz + z, c),
        )

    near = sorted(range(1, nz), key=lambda d: min(d, nz - d))

    def wait_sends(t, s):
        for dz in range(nz):
            if dz:
                z_copy(t, s, dz).wait_send()
            for dy in range(1, ny):
                y_copy(t, s, dz, dy).wait_send()

    def arrived(t, s, tile):
        remote(gath.at[t, tile], gath.at[t, tile], z_send.at[s, 0], g_recv.at[s, tile], dev(r, m, other)).wait_recv()

    def block(t, p, row):
        x = jnp.concatenate([gath[t, row * nz + i] for i in range(nz)], axis=1)
        cols = pl.ds(pl.multiple_of(row * (nz * 128), nz * 128), nz * 128)
        return dot(x, tops[p, :, cols], NT)

    def solve(t, p, value, extra):
        s = lax.rem(t, 2)
        gath[t, m] = value
        for dz in reversed(near):
            z_copy(t, s, dz).start()
        for dy in range(1, ny):
            y_copy(t, s, 0, dy).start()
        extra()
        for dz in near:
            arrived(t, s, y * nz + lax.rem(z + dz, nz))
            for dy in range(1, ny):
                y_copy(t, s, dz, dy).start()
        total = block(t, p, y)
        for dy in range(1, ny):
            row = lax.rem(y + dy, ny)
            for i in range(nz):
                arrived(t, s, row * nz + lax.rem(z + i, nz))
            total += block(t, p, row)
        return total

    def send_field(p, value):
        field[p] = value.astype(BF)
        mine = r * 2 + c

        @pl.when(p == r)
        def _():
            own_w[mine] = value.astype(BF)

        @pl.when(p != r)
        def _():
            remote(field.at[p], own_w.at[mine], o_send.at[p, 0], o_recv.at[mine, 0], dev(p, m, c)).start()

        for copy in field_copies(p):
            copy.start()

    def field_copies(p):
        mine = r * 2 + c
        return [
            remote(field.at[p], own_w.at[mine], o_send.at[p, 1], o_recv.at[mine, 0], dev(p, m, other)),
            remote(field.at[p], nb_w.at[mine], o_send.at[p, 2], o_recv.at[mine, 1], dev(p, down, 1)),
            remote(field.at[p], nb_w.at[mine], o_send.at[p, 3], o_recv.at[mine, 1], dev(p, up, 0)),
        ]

    tabs[12] = jnp.zeros((GROUP, 128), F32)

    def forward(t, carry):
        meet_pieces(t)
        value = (tabs[t] + tabs[4 + t] * tabs[12]).astype(BF)

        def extra():
            @pl.when(t == 0)
            def _():
                for k, copy in enumerate(piece_sends):
                    copy.wait_send()

            @pl.when(t > 0)
            def _():
                wait_sends(t - 1, lax.rem(t + 1, 2))

        def first():
            @pl.when(t == 0)
            def _():
                finish_tops()

        top = solve_with(t, t, value, extra, first).astype(BF).astype(F32)
        tabs[8 + t] = top
        tabs[12] = top
        return carry

    def solve_with(t, p, value, extra, first):
        def both():
            extra()
            first()

        return solve(t, p, value, both)

    lax.fori_loop(0, panels, forward, 0)

    nothing = jnp.zeros((GROUP, chips * 128), BF)
    fix = dot(nothing, tops[3], NT).astype(BF).astype(F32)
    top = (tabs[12] + fix).astype(BF).astype(F32)
    tabs[12] = top
    send_field(jnp.int32(3), top)

    def backward(t, carry):
        p = 6 - t
        value = (tabs[5 + p] * tabs[12]).astype(BF)
        fixed = solve(t, p, value, lambda: wait_sends(t - 1, lax.rem(t + 1, 2))).astype(BF).astype(F32)
        top = (tabs[8 + p] + fixed).astype(BF).astype(F32)
        tabs[12] = top
        send_field(p, top)
        return carry

    lax.fori_loop(4, STEPS, backward, 0)
    wait_sends(STEPS - 1, (STEPS - 1) % 2)

    for k in range(8):
        @pl.when(k != r * 2 + c)
        def _():
            remote(field.at[0], own_w.at[k], o_send.at[0, 0], o_recv.at[k, 0], dev(r, m, other)).wait_recv()

        remote(field.at[0], nb_w.at[k], o_send.at[0, 0], o_recv.at[k, 1], dev(r, m, other)).wait_recv()
    for p in range(panels):
        @pl.when(p != r)
        def _():
            remote(field.at[p], own_w.at[0], o_send.at[p, 0], o_recv.at[0, 0], dev(r, m, other)).wait_send()

        for copy in field_copies(p):
            copy.wait_send()

    own = own_w[...].reshape(128, 128)
    window = jnp.concatenate([own, nb_w[...].reshape(128, 128)], axis=1)
    half[...] = jnp.where(c == 0, own[:, :64], own[:, 64:])
    top_out = pltpu.make_async_copy(half, tf_hbm.at[0], out_sem.at[chunks])
    top_out.start()
    outs = []
    for g in range(chunks):
        cols = slice(g * per * width, (g + 1) * per * width)
        vec[:, cols] = (inner[:, cols].astype(F32) - dot(window, lift[:, cols], NN)).astype(BF)
        outs.append(pltpu.make_async_copy(vec.at[:, cols], lf_hbm.at[0, :, cols], out_sem.at[g]))
        outs[-1].start()
    for copy in outs:
        copy.wait()
    top_out.wait()


def body(sizes, top_source, leaf_source, top_inverse, leaf_inverse, boundary, touch_rows, coupling):
    ny, nz, chunks, per = sizes
    leaves, width = leaf_inverse.shape[1:3]
    reach = boundary.shape[2]
    columns = leaves * width
    order = ny * nz * 128
    any_spec = pl.BlockSpec(memory_space=pl.ANY)
    dma = pltpu.SemaphoreType.DMA
    vmem = pltpu.VMEM
    return pl.pallas_call(
        functools.partial(kernel, sizes),
        out_shape=(
            jax.ShapeDtypeStruct(top_source.shape, BF),
            jax.ShapeDtypeStruct(leaf_source.shape, BF),
        ),
        in_specs=[any_spec] * 7,
        out_specs=(any_spec, any_spec),
        scratch_shapes=[
            vmem((128, 64), BF),
            vmem((128, columns), BF),
            vmem((leaves, width, width), BF),
            vmem((leaves, reach, width), BF),
            vmem((leaves, reach), jnp.int32),
            vmem((1, 64), F32),
            vmem((128, columns), BF),
            vmem((256, columns), BF),
            vmem((128, 256), F32),
            vmem((8, GROUP + 8, 128), F32),
            vmem((8, GROUP, 128), F32),
            vmem((4, 2, GROUP + 8, 128), F32),
            vmem((4, 2, GROUP, 128), F32),
            vmem((4, 128, order), BF),
            vmem((STEPS, ny * nz, GROUP, 128), BF),
            vmem((16, GROUP, 128), F32),
            vmem((4, GROUP, 128), BF),
            vmem((8, GROUP, 128), BF),
            vmem((8, GROUP, 128), BF),
            vmem((128, 64), BF),
            dma((3, chunks)), dma((4,)), dma((chunks + 1,)),
            dma((4,)), dma((4,)), dma((4,)), dma((4,)),
            dma((8,)), dma((4, 2)), dma((8,)), dma((4, 2)),
            dma((2, nz - 1)), dma((2, nz, ny - 1)), dma((2, ny * nz)),
            dma((4, 4)), dma((8, 2)),
        ],
        compiler_params=pltpu.CompilerParams(
            collective_id=0, has_side_effects=True, vmem_limit_bytes=50 * 1024 * 1024
        ),
    )(top_source, leaf_source, top_inverse, leaf_inverse, boundary, touch_rows, coupling)


def solution(mesh, sizes=(4, 8, 6, 6)):
    placed = (
        P("panel", None, "front"),
        P("panel", None, "front"),
        P("panel", "front", None),
        P("panel", "front", None, None),
        P("panel", "front", None, None),
        P("panel", "front", None),
        P("panel", "front"),
    )
    return jax.shard_map(
        functools.partial(body, sizes),
        mesh=mesh,
        in_specs=placed,
        out_specs=(P("panel", None, "front"), P("panel", None, "front")),
        check_vma=False,
    )
```

```python
import functools

import jax
import jax.numpy as jnp
from jax import lax
from jax.experimental import pallas as pl
from jax.experimental.pallas import tpu as pltpu
from jax.sharding import PartitionSpec as P

MESH = pl.DeviceIdType.MESH
BF = jnp.bfloat16
F32 = jnp.float32
NT = (((1,), (1,)), ((), ()))
NN = (((1,), (0,)), ((), ()))
STEPS = 7
GROUP = 16


def dot(a, b, dims):
    return lax.dot_general(a, b, dims, preferred_element_type=F32)


def kernel(
    sizes,
    ts_hbm, ls_hbm, ti_hbm, li_hbm, bd_hbm, tr_hbm, cp_hbm,
    tf_hbm, lf_hbm,
    ts, vec, inv, bnd, rows, cpl,
    inner, lift, acc, main, halo, main_in, halo_in, tops, gath, tabs, field, own_w, nb_w, half,
    in_sem, small_sem, out_sem,
    ta_send, ta_recv, tc_send, tc_recv,
    pm_send, pm_recv, ph_send, ph_recv,
    g_send, g_recv, o_send, o_recv,
):
    ny, nz, chunks, per = sizes
    chips = ny * nz
    panels = 4
    r = lax.axis_index("panel")
    f = lax.axis_index("front")
    m, c = lax.div(f, 2), lax.rem(f, 2)
    y, z = lax.div(m, nz), lax.rem(m, nz)
    other = 1 - c
    up, down = lax.rem(m + 1, chips), lax.rem(m + chips - 1, chips)
    side = lax.rem(m + chips - 1 + 2 * c, chips)

    def dev(q, chip, core):
        return (q, chip * 2 + core)

    def chip_at(dy, dz):
        return lax.rem(y + dy, ny) * nz + lax.rem(z + dz, nz)

    steps_away = sorted(
        ((dy, dz) for dy in range(ny) for dz in range(nz) if dy or dz),
        key=lambda d: -min(d[0], ny - d[0]) - min(d[1], nz - d[1]),
    )

    def remote(src, dst, send, recv, where):
        return pltpu.make_async_remote_copy(
            src_ref=src, dst_ref=dst, send_sem=send, recv_sem=recv,
            device_id=where, device_id_type=MESH,
        )

    width = ls_hbm.shape[2] // chunks // per

    small = [
        pltpu.make_async_copy(ts_hbm.at[0], ts, small_sem.at[0]),
        pltpu.make_async_copy(tr_hbm, rows, small_sem.at[1]),
        pltpu.make_async_copy(cp_hbm, cpl, small_sem.at[2]),
        pltpu.make_async_copy(
            ti_hbm.at[0], tops.at[r, pl.ds(pl.multiple_of(c * 64, 64), 64)], small_sem.at[3]
        ),
    ]

    def big(g):
        at = pl.ds(g * per, per)
        cols = pl.ds(pl.multiple_of(g * (per * width), per * width), per * width)
        return (
            pltpu.make_async_copy(ls_hbm.at[0, :, cols], vec.at[:, cols], in_sem.at[2, g]),
            pltpu.make_async_copy(li_hbm.at[0, at], inv.at[at], in_sem.at[1, g]),
            pltpu.make_async_copy(bd_hbm.at[0, at], bnd.at[at], in_sem.at[0, g]),
        )

    small[1].start()
    for copy in big(0):
        copy.start()
    for copy in (small[0], small[2], small[3]):
        copy.start()
    for g in range(1, chunks):
        for copy in big(g):
            copy.start()

    barrier = pltpu.get_barrier_semaphore()
    peers = [dev(r, chip_at(dy, dz), c) for dy, dz in steps_away]
    beyond = lax.rem(m + chips + 1 - 2 * c, chips)
    for dq in range(panels):
        q = lax.rem(r + dq, panels)
        if dq:
            peers += [dev(q, m, c), dev(q, side, c), dev(q, beyond, c)]
        peers += [dev(q, m, other), dev(q, side, other)]
    for peer in peers:
        pl.semaphore_signal(barrier, inc=1, device_id=peer, device_id_type=MESH)

    acc[...] = jnp.zeros_like(acc)
    base = m * 128
    small[1].wait()

    def columns_of(j):
        return pl.ds(pl.multiple_of(j * width, width), width)

    def hot_rows(j):
        u = jnp.bitwise_and(rows[j] - base, 255)
        hot = lax.broadcasted_iota(jnp.int32, (256, u.shape[1]), 0) == u
        return jnp.where(hot, 1.0, 0.0).astype(BF)

    def leaf(j):
        solved = dot(vec[:, columns_of(j)], inv[j], NT).astype(BF)
        inner[:, columns_of(j)] = solved
        return dot(solved, bnd[j], NT).astype(BF)

    def leaves(g, carry):
        for copy in big(g):
            copy.wait()
        first = g * per
        pushed = jnp.concatenate([leaf(first + i) for i in range(per)], axis=1)
        hot = jnp.concatenate([hot_rows(first + i) for i in range(per)], axis=1)
        acc[...] += dot(pushed, hot, NT)
        return carry

    def lifts(g):
        for i in range(per):
            j = g * per + i
            spread = dot(hot_rows(j), bnd[j], NN).astype(BF)
            lift[:, columns_of(j)] = dot(spread, inv[j], NT).astype(BF)

    early = chunks // 3
    lax.fori_loop(0, early, leaves, 0)
    pl.semaphore_wait(barrier, len(peers))

    right, left, far = lax.rem(r + 1, 4), lax.rem(r + 3, 4), lax.rem(r + 2, 4)

    def rows_of(q, core, start=0, size=32):
        return tops.at[q, pl.ds(pl.multiple_of(core * 64 + start, 32), size)]

    def across(n, q, start, to, fresh):
        dst = rows_of(q, c, start)
        src = ti_hbm.at[0, pl.ds(start, 32)] if fresh else dst
        return remote(src, dst, ta_send.at[n], ta_recv.at[n], dev(to, m, c))

    def share(n, q, start, size=32):
        part = rows_of(q, c, start, size)
        src = ti_hbm.at[0] if size == 64 else part
        return remote(src, part, tc_send.at[n], tc_recv.at[n], dev(r, m, other))

    first_right, first_left = across(0, r, 0, right, True), across(1, r, 32, left, True)
    second_right, second_left = across(2, r, 32, right, True), across(3, r, 0, left, True)
    on_right, on_left = across(4, left, 0, right, False), across(5, right, 32, left, False)
    shares = [
        share(0, r, 0, 64), share(1, left, 0), share(2, right, 32), share(3, left, 32),
        share(4, right, 0), share(5, far, 0), share(6, far, 32),
    ]
    first_right.start()
    first_left.start()
    shares[0].start()

    lax.fori_loop(early, chunks, leaves, 0)

    for k in (0, 2):
        small[k].wait()
    known = -acc[:, :128]
    local = ts[...].astype(F32)
    zero = jnp.zeros_like(local)
    lower = jnp.where(c == 0, local, zero)
    upper = jnp.where(c == 0, zero, local)
    known = known + jnp.transpose(jnp.concatenate([lower, upper], axis=0))
    scale = cpl[...]
    blank = jnp.zeros_like(scale)
    scale = jnp.concatenate(
        [jnp.where(c == 0, scale, blank), jnp.where(c == 0, blank, scale)], axis=1
    )
    scale = jnp.broadcast_to(scale, (8, 128))
    for k in range(8):
        main[k, :GROUP] = known[k * GROUP : (k + 1) * GROUP]
        main[k, GROUP:] = scale
        halo[k] = -acc[k * GROUP : (k + 1) * GROUP, 128:]
    mine = r * 2 + c
    main_in[r, c] = main[mine]

    piece_sends = []
    for dq in range(panels):
        q = lax.rem(r + dq, panels)
        for n, core in enumerate((c, other)):
            k, slot = q * 2 + core, dq * 2 + n
            if slot:
                piece_sends.append(remote(
                    main.at[k], main_in.at[r, c], pm_send.at[slot], pm_recv.at[r, c], dev(q, m, core)
                ))
            piece_sends.append(remote(
                halo.at[k], halo_in.at[r, c], ph_send.at[slot], ph_recv.at[r, c], dev(q, side, core)
            ))
    for copy in piece_sends:
        copy.start()

    @pl.when(r == 0)
    def _():
        second_right.start()

    @pl.when(r < 3)
    def _():
        second_left.start()

    first_right.wait_recv()
    on_right.start()
    shares[1].start()
    first_left.wait_recv()
    on_left.start()
    shares[2].start()

    @pl.when(r > 0)
    def _():
        second_right.start()

    @pl.when(r == 3)
    def _():
        second_left.start()

    def meet_tops(t):
        away = lax.rem(t + panels - r, panels)

        @pl.when(away == 0)
        def _():
            small[3].wait()
            shares[0].wait_recv()

        @pl.when(away == 1)
        def _():
            second_left.wait_recv()
            shares[4].start()
            shares[2].wait_recv()
            shares[4].wait_recv()

        @pl.when(away == 2)
        def _():
            on_right.wait_recv()
            shares[5].start()
            on_left.wait_recv()
            shares[6].start()
            shares[5].wait_recv()
            shares[6].wait_recv()

        @pl.when(away == 3)
        def _():
            second_right.wait_recv()
            shares[3].start()
            shares[1].wait_recv()
            shares[3].wait_recv()

    def meet_pieces(p):
        for core in (0, 1):
            arrival = remote(main.at[0], main_in.at[p, core], pm_send.at[0], pm_recv.at[p, core], dev(r, m, other))

            @pl.when(jnp.logical_or(p != r, c != core))
            def _():
                arrival.wait_recv()

            remote(halo.at[0], halo_in.at[p, core], ph_send.at[0], ph_recv.at[p, core], dev(r, m, other)).wait_recv()
        a, b = main_in[p, 0], main_in[p, 1]
        tabs[p] = a[:GROUP] + b[:GROUP] + halo_in[p, 0] + halo_in[p, 1]
        pair = a[GROUP:] + b[GROUP:]
        tabs[4 + p] = jnp.concatenate([pair, pair], axis=0)

    def sends(t, s):
        return [
            remote(gath.at[t, m], gath.at[t, m], g_send.at[s, n], g_recv.at[s, m], dev(r, chip_at(dy, dz), c))
            for n, (dy, dz) in enumerate(steps_away)
        ]

    def wait_sends(t, s):
        for copy in sends(t, s):
            copy.wait_send()

    def arrived(t, s, tile):
        remote(gath.at[t, tile], gath.at[t, tile], g_send.at[s, 0], g_recv.at[s, tile], dev(r, m, other)).wait_recv()

    def solve(t, p, value, meanwhile):
        s = lax.rem(t, 2)
        gath[t, m] = value
        for copy in sends(t, s):
            copy.start()
        meanwhile()
        total = jnp.zeros((GROUP, 128), F32)
        for dy in sorted(range(ny), key=lambda d: min(d, ny - d)):
            row = lax.rem(y + dy, ny)
            for dz in range(nz):
                if dy or dz:
                    arrived(t, s, row * nz + lax.rem(z + dz, nz))
            x = jnp.concatenate([gath[t, row * nz + i] for i in range(nz)], axis=1)
            cols = pl.ds(pl.multiple_of(row * (nz * 128), nz * 128), nz * 128)
            total += dot(x, tops[p, :, cols], NT)
        return total

    def send_field(p, value):
        field[p] = value.astype(BF)
        mine = r * 2 + c

        @pl.when(p == r)
        def _():
            own_w[mine] = value.astype(BF)

        @pl.when(p != r)
        def _():
            remote(field.at[p], own_w.at[mine], o_send.at[p, 0], o_recv.at[mine, 0], dev(p, m, c)).start()

        for copy in field_copies(p):
            copy.start()

    def field_copies(p):
        mine = r * 2 + c
        return [
            remote(field.at[p], own_w.at[mine], o_send.at[p, 1], o_recv.at[mine, 0], dev(p, m, other)),
            remote(field.at[p], nb_w.at[mine], o_send.at[p, 2], o_recv.at[mine, 1], dev(p, down, 1)),
            remote(field.at[p], nb_w.at[mine], o_send.at[p, 3], o_recv.at[mine, 1], dev(p, up, 0)),
        ]

    tabs[12] = jnp.zeros((GROUP, 128), F32)

    def forward(t, carry):
        meet_pieces(t)
        value = (tabs[t] + tabs[4 + t] * tabs[12]).astype(BF)

        def meanwhile():
            @pl.when(t > 0)
            def _():
                wait_sends(t - 1, lax.rem(t + 1, 2))

            lifts(t)
            meet_tops(t)

        top = solve(t, t, value, meanwhile).astype(BF).astype(F32)
        tabs[8 + t] = top
        tabs[12] = top
        return carry

    lax.fori_loop(0, panels, forward, 0)

    nothing = jnp.zeros((GROUP, chips * 128), BF)
    fix = dot(nothing, tops[3], NT).astype(BF).astype(F32)
    top = (tabs[12] + fix).astype(BF).astype(F32)
    tabs[12] = top
    send_field(jnp.int32(3), top)

    def backward(t, carry):
        p = 6 - t
        value = (tabs[5 + p] * tabs[12]).astype(BF)

        def meanwhile():
            wait_sends(t - 1, lax.rem(t + 1, 2))

            @pl.when(t < chunks)
            def _():
                lifts(t)

        fixed = solve(t, p, value, meanwhile).astype(BF).astype(F32)
        top = (tabs[8 + p] + fixed).astype(BF).astype(F32)
        tabs[12] = top
        send_field(p, top)
        return carry

    lax.fori_loop(4, STEPS, backward, 0)
    wait_sends(STEPS - 1, (STEPS - 1) % 2)
    crossed = [first_right, first_left, second_right, second_left, on_right, on_left]
    for copy in piece_sends + crossed + shares:
        copy.wait_send()

    for k in range(8):
        @pl.when(k != r * 2 + c)
        def _():
            remote(field.at[0], own_w.at[k], o_send.at[0, 0], o_recv.at[k, 0], dev(r, m, other)).wait_recv()

        remote(field.at[0], nb_w.at[k], o_send.at[0, 0], o_recv.at[k, 1], dev(r, m, other)).wait_recv()
    for p in range(panels):
        @pl.when(p != r)
        def _():
            remote(field.at[p], own_w.at[0], o_send.at[p, 0], o_recv.at[0, 0], dev(r, m, other)).wait_send()

        for copy in field_copies(p):
            copy.wait_send()

    own = own_w[...].reshape(128, 128)
    window = jnp.concatenate([own, nb_w[...].reshape(128, 128)], axis=1)
    turned = jnp.transpose(own.astype(F32))
    half[...] = jnp.where(c == 0, turned[:64], turned[64:]).astype(BF)
    top_out = pltpu.make_async_copy(half, tf_hbm.at[0], out_sem.at[chunks])
    top_out.start()
    outs = []
    for g in range(chunks):
        cols = slice(g * per * width, (g + 1) * per * width)
        vec[:, cols] = (inner[:, cols].astype(F32) - dot(window, lift[:, cols], NN)).astype(BF)
        outs.append(pltpu.make_async_copy(vec.at[:, cols], lf_hbm.at[0, :, cols], out_sem.at[g]))
        outs[-1].start()
    for copy in outs:
        copy.wait()
    top_out.wait()


def body(sizes, top_source, leaf_source, top_inverse, leaf_inverse, boundary, touch_rows, coupling):
    ny, nz, chunks, per = sizes
    leaves, width = leaf_inverse.shape[1:3]
    reach = boundary.shape[2]
    columns = leaves * width
    order = ny * nz * 128
    any_spec = pl.BlockSpec(memory_space=pl.ANY)
    hbm_spec = pl.BlockSpec(memory_space=pltpu.HBM)
    dma = pltpu.SemaphoreType.DMA
    vmem = pltpu.VMEM
    top, leaf = pl.pallas_call(
        functools.partial(kernel, sizes),
        out_shape=(
            jax.ShapeDtypeStruct((1, 64, 128), BF),
            jax.ShapeDtypeStruct(leaf_source.shape, BF),
        ),
        in_specs=[hbm_spec] * 7,
        out_specs=(any_spec, any_spec),
        scratch_shapes=[
            vmem((64, 128), BF),
            vmem((128, columns), BF),
            vmem((leaves, width, width), BF),
            vmem((leaves, reach, width), BF),
            vmem((leaves, 1, reach), jnp.int32),
            vmem((1, 64), F32),
            vmem((128, columns), BF),
            vmem((256, columns), BF),
            vmem((128, 256), F32),
            vmem((8, GROUP + 8, 128), F32),
            vmem((8, GROUP, 128), F32),
            vmem((4, 2, GROUP + 8, 128), F32),
            vmem((4, 2, GROUP, 128), F32),
            vmem((4, 128, order), BF),
            vmem((STEPS, ny * nz, GROUP, 128), BF),
            vmem((16, GROUP, 128), F32),
            vmem((4, GROUP, 128), BF),
            vmem((8, GROUP, 128), BF),
            vmem((8, GROUP, 128), BF),
            vmem((64, 128), BF),
            dma((3, chunks)), dma((4,)), dma((chunks + 1,)),
            dma((6,)), dma((6,)), dma((7,)), dma((7,)),
            dma((8,)), dma((4, 2)), dma((8,)), dma((4, 2)),
            dma((2, ny * nz - 1)), dma((2, ny * nz)),
            dma((4, 4)), dma((8, 2)),
        ],
        compiler_params=pltpu.CompilerParams(
            collective_id=0, has_side_effects=True, vmem_limit_bytes=50 * 1024 * 1024
        ),
    )(
        jnp.swapaxes(top_source, 1, 2), leaf_source, top_inverse, leaf_inverse, boundary,
        jnp.swapaxes(touch_rows, 0, 1), coupling,
    )
    return jnp.swapaxes(top, 1, 2), leaf


def solution(mesh, sizes=(4, 8, 6, 6)):
    placed = (
        P("panel", None, "front"),
        P("panel", None, "front"),
        P("panel", "front", None),
        P("panel", "front", None, None),
        P("panel", "front", None, None),
        P("panel", "front", None),
        P("panel", "front"),
    )
    return jax.shard_map(
        functools.partial(body, sizes),
        mesh=mesh,
        in_specs=placed,
        out_specs=(P("panel", None, "front"), P("panel", None, "front")),
        check_vma=False,
    )
```

```python
import functools

import jax
import jax.numpy as jnp
from jax import lax
from jax.experimental import pallas as pl
from jax.experimental.pallas import tpu as pltpu
from jax.sharding import PartitionSpec as P

MESH = pl.DeviceIdType.MESH
BF = jnp.bfloat16
F32 = jnp.float32
NT = (((1,), (1,)), ((), ()))
NN = (((1,), (0,)), ((), ()))
STEPS = 7
GROUP = 16


def dot(a, b, dims):
    return lax.dot_general(a, b, dims, preferred_element_type=F32)


def kernel(
    sizes,
    ts_hbm, ls_hbm, ti_hbm, li_hbm, bd_hbm, tr_hbm, cp_hbm,
    tf_hbm, lf_hbm,
    ts, vec, inv, bnd, rows, cpl,
    inner, lift, acc, main, halo, main_in, halo_in, scale, scale_in, tops, gath, tabs, field, own_w, nb_w, half,
    in_sem, small_sem, out_sem,
    ta_send, ta_recv, tc_send, tc_recv,
    pm_send, pm_recv, ph_send, ph_recv, pc_send, pc_recv,
    g_send, g_recv, o_send, o_recv,
):
    ny, nz, chunks, per = sizes
    chips = ny * nz
    panels = 4
    r = lax.axis_index("panel")
    f = lax.axis_index("front")
    m, c = lax.div(f, 2), lax.rem(f, 2)
    y, z = lax.div(m, nz), lax.rem(m, nz)
    other = 1 - c
    up, down = lax.rem(m + 1, chips), lax.rem(m + chips - 1, chips)
    side = lax.rem(m + chips - 1 + 2 * c, chips)

    def dev(q, chip, core):
        return (q, chip * 2 + core)

    def chip_at(dy, dz):
        return lax.rem(y + dy, ny) * nz + lax.rem(z + dz, nz)

    steps_away = sorted(
        ((dy, dz) for dy in range(ny) for dz in range(nz) if dy or dz),
        key=lambda d: -min(d[0], ny - d[0]) - min(d[1], nz - d[1]),
    )

    def remote(src, dst, send, recv, where):
        return pltpu.make_async_remote_copy(
            src_ref=src, dst_ref=dst, send_sem=send, recv_sem=recv,
            device_id=where, device_id_type=MESH,
        )

    width = ls_hbm.shape[2] // chunks // per

    small = [
        pltpu.make_async_copy(ts_hbm.at[0], ts, small_sem.at[0]),
        pltpu.make_async_copy(tr_hbm, rows, small_sem.at[1]),
        pltpu.make_async_copy(cp_hbm, cpl, small_sem.at[2]),
        pltpu.make_async_copy(
            ti_hbm.at[0], tops.at[r, pl.ds(pl.multiple_of(c * 64, 64), 64)], small_sem.at[3]
        ),
    ]

    def big(g):
        at = pl.ds(g * per, per)
        cols = pl.ds(pl.multiple_of(g * (per * width), per * width), per * width)
        return (
            pltpu.make_async_copy(ls_hbm.at[0, :, cols], vec.at[:, cols], in_sem.at[2, g]),
            pltpu.make_async_copy(li_hbm.at[0, at], inv.at[at], in_sem.at[1, g]),
            pltpu.make_async_copy(bd_hbm.at[0, at], bnd.at[at], in_sem.at[0, g]),
        )

    small[1].start()
    for copy in big(0):
        copy.start()
    for copy in (small[0], small[2], small[3]):
        copy.start()
    for g in range(1, chunks):
        for copy in big(g):
            copy.start()

    barrier = pltpu.get_barrier_semaphore()
    peers = [dev(r, chip_at(dy, dz), c) for dy, dz in steps_away]
    beyond = lax.rem(m + chips + 1 - 2 * c, chips)
    for dq in range(panels):
        q = lax.rem(r + dq, panels)
        if dq:
            peers += [dev(q, m, c), dev(q, side, c), dev(q, beyond, c)]
        peers += [dev(q, m, other), dev(q, side, other)]
    for peer in peers:
        pl.semaphore_signal(barrier, inc=1, device_id=peer, device_id_type=MESH)

    acc[...] = jnp.zeros_like(acc)
    base = m * 128
    small[1].wait()

    def columns_of(j):
        return pl.ds(pl.multiple_of(j * width, width), width)

    def hot_rows(j):
        u = jnp.bitwise_and(rows[j] - base, 255)
        hot = lax.broadcasted_iota(jnp.int32, (256, u.shape[1]), 0) == u
        return jnp.where(hot, 1.0, 0.0).astype(BF)

    def leaf(j):
        solved = dot(vec[:, columns_of(j)], inv[j], NT).astype(BF)
        inner[:, columns_of(j)] = solved
        return dot(solved, bnd[j], NT).astype(BF)

    def leaves(g, carry):
        for copy in big(g):
            copy.wait()
        first = g * per
        pushed = jnp.concatenate([leaf(first + i) for i in range(per)], axis=1)
        hot = jnp.concatenate([hot_rows(first + i) for i in range(per)], axis=1)
        acc[...] += dot(pushed, hot, NT)
        return carry

    def lifts(g):
        for i in range(per):
            j = g * per + i
            spread = dot(hot_rows(j), bnd[j], NN).astype(BF)
            lift[:, columns_of(j)] = dot(spread, inv[j], NT).astype(BF)

    early = 1
    lax.fori_loop(0, early, leaves, 0)
    pl.semaphore_wait(barrier, len(peers))

    right, left, far = lax.rem(r + 1, 4), lax.rem(r + 3, 4), lax.rem(r + 2, 4)

    def rows_of(q, core, start=0, size=32):
        return tops.at[q, pl.ds(pl.multiple_of(core * 64 + start, 32), size)]

    def across(n, q, start, to, fresh):
        dst = rows_of(q, c, start)
        src = ti_hbm.at[0, pl.ds(start, 32)] if fresh else dst
        return remote(src, dst, ta_send.at[n], ta_recv.at[n], dev(to, m, c))

    def share(n, q, start, size=32):
        part = rows_of(q, c, start, size)
        src = ti_hbm.at[0] if size == 64 else part
        return remote(src, part, tc_send.at[n], tc_recv.at[n], dev(r, m, other))

    first_right, first_left = across(0, r, 0, right, True), across(1, r, 32, left, True)
    second_right, second_left = across(2, r, 32, right, True), across(3, r, 0, left, True)
    on_right, on_left = across(4, left, 0, right, False), across(5, right, 32, left, False)
    shares = [
        share(0, r, 0, 64), share(1, left, 0), share(2, right, 32), share(3, left, 32),
        share(4, right, 0), share(5, far, 0), share(6, far, 32),
    ]
    small[2].wait()
    own_scale = cpl[...]
    blank = jnp.zeros_like(own_scale)
    own_scale = jnp.concatenate(
        [jnp.where(c == 0, own_scale, blank), jnp.where(c == 0, blank, own_scale)], axis=1
    )
    scale[...] = jnp.broadcast_to(own_scale, scale.shape)
    scale_in[r, c] = scale[...]
    scale_sends = []
    for dq in range(panels):
        q = lax.rem(r + dq, panels)
        for n, core in enumerate((c, other)):
            if dq or n:
                scale_sends.append(remote(
                    scale, scale_in.at[r, c], pc_send.at[dq * 2 + n], pc_recv.at[r, c], dev(q, m, core)
                ))
    for copy in scale_sends:
        copy.start()
    first_right.start()
    first_left.start()
    shares[0].start()

    lax.fori_loop(early, chunks, leaves, 0)

    small[0].wait()
    known = -acc[:, :128]
    local = ts[...].astype(F32)
    zero = jnp.zeros_like(local)
    lower = jnp.where(c == 0, local, zero)
    upper = jnp.where(c == 0, zero, local)
    known = known + jnp.transpose(jnp.concatenate([lower, upper], axis=0))
    for k in range(8):
        main[k] = known[k * GROUP : (k + 1) * GROUP].astype(BF)
        halo[k] = (-acc[k * GROUP : (k + 1) * GROUP, 128:]).astype(BF)
    mine = r * 2 + c
    main_in[r, c] = main[mine]

    piece_sends = []
    for dq in range(panels):
        q = lax.rem(r + dq, panels)
        for n, core in enumerate((c, other)):
            k, slot = q * 2 + core, dq * 2 + n
            if slot:
                piece_sends.append(remote(
                    main.at[k], main_in.at[r, c], pm_send.at[slot], pm_recv.at[r, c], dev(q, m, core)
                ))
            piece_sends.append(remote(
                halo.at[k], halo_in.at[r, c], ph_send.at[slot], ph_recv.at[r, c], dev(q, side, core)
            ))
    for copy in piece_sends:
        copy.start()

    @pl.when(r == 0)
    def _():
        second_right.start()

    @pl.when(r < 3)
    def _():
        second_left.start()

    first_right.wait_recv()
    on_right.start()
    shares[1].start()
    first_left.wait_recv()
    on_left.start()
    shares[2].start()

    @pl.when(r > 0)
    def _():
        second_right.start()

    @pl.when(r == 3)
    def _():
        second_left.start()

    def meet_tops(t):
        away = lax.rem(t + panels - r, panels)

        @pl.when(away == 0)
        def _():
            small[3].wait()
            shares[0].wait_recv()

        @pl.when(away == 1)
        def _():
            second_left.wait_recv()
            shares[4].start()
            shares[2].wait_recv()
            shares[4].wait_recv()

        @pl.when(away == 2)
        def _():
            on_right.wait_recv()
            shares[5].start()
            on_left.wait_recv()
            shares[6].start()
            shares[5].wait_recv()
            shares[6].wait_recv()

        @pl.when(away == 3)
        def _():
            second_right.wait_recv()
            shares[3].start()
            shares[1].wait_recv()
            shares[3].wait_recv()

    def meet_pieces(p):
        for core in (0, 1):
            for_main = remote(main.at[0], main_in.at[p, core], pm_send.at[0], pm_recv.at[p, core], dev(r, m, other))
            for_scale = remote(scale, scale_in.at[p, core], pc_send.at[0], pc_recv.at[p, core], dev(r, m, other))

            @pl.when(jnp.logical_or(p != r, c != core))
            def _():
                for_scale.wait_recv()
                for_main.wait_recv()

            remote(halo.at[0], halo_in.at[p, core], ph_send.at[0], ph_recv.at[p, core], dev(r, m, other)).wait_recv()
        terms = [ref[p, core].astype(F32) for ref in (main_in, halo_in) for core in (0, 1)]
        tabs[p] = (terms[0] + terms[1]) + (terms[2] + terms[3])
        pair = scale_in[p, 0] + scale_in[p, 1]
        tabs[4 + p] = jnp.concatenate([pair, pair], axis=0)

    def sends(t, s):
        return [
            remote(gath.at[t, m], gath.at[t, m], g_send.at[s, n], g_recv.at[s, m], dev(r, chip_at(dy, dz), c))
            for n, (dy, dz) in enumerate(steps_away)
        ]

    def wait_sends(t, s):
        for copy in sends(t, s):
            copy.wait_send()

    def arrived(t, s, tile):
        remote(gath.at[t, tile], gath.at[t, tile], g_send.at[s, 0], g_recv.at[s, tile], dev(r, m, other)).wait_recv()

    def solve(t, p, value, meanwhile):
        s = lax.rem(t, 2)
        gath[t, m] = value
        for copy in sends(t, s):
            copy.start()
        meanwhile()
        total = jnp.zeros((GROUP, 128), F32)
        nearest = [(0, 0)] + steps_away[::-1]
        cuts = sorted({0} | {len(nearest) * k // 16 for k in (4, 8, 12, 15, 16)})
        for low, high in zip(cuts, cuts[1:]):
            tiles = [chip_at(dy, dz) for dy, dz in nearest[low:high]]
            for n, tile in enumerate(tiles):
                if low + n:
                    arrived(t, s, tile)
            x = jnp.concatenate([gath[t, tile] for tile in tiles], axis=1)
            w = [tops[p, :, pl.ds(pl.multiple_of(tile * 128, 128), 128)] for tile in tiles]
            total += dot(x, jnp.concatenate(w, axis=1), NT)
        return total

    def send_field(p, value):
        field[p] = value.astype(BF)
        mine = r * 2 + c

        @pl.when(p == r)
        def _():
            own_w[mine] = value.astype(BF)

        @pl.when(p != r)
        def _():
            remote(field.at[p], own_w.at[mine], o_send.at[p, 0], o_recv.at[mine, 0], dev(p, m, c)).start()

        for copy in field_copies(p):
            copy.start()

    def field_copies(p):
        mine = r * 2 + c
        return [
            remote(field.at[p], own_w.at[mine], o_send.at[p, 1], o_recv.at[mine, 0], dev(p, m, other)),
            remote(field.at[p], nb_w.at[mine], o_send.at[p, 2], o_recv.at[mine, 1], dev(p, down, 1)),
            remote(field.at[p], nb_w.at[mine], o_send.at[p, 3], o_recv.at[mine, 1], dev(p, up, 0)),
        ]

    tabs[12] = jnp.zeros((GROUP, 128), F32)

    def forward(t, carry):
        meet_pieces(t)
        value = (tabs[t] + tabs[4 + t] * tabs[12]).astype(BF)

        def meanwhile():
            @pl.when(t > 0)
            def _():
                wait_sends(t - 1, lax.rem(t + 1, 2))

            lifts(t)
            meet_tops(t)

        top = solve(t, t, value, meanwhile).astype(BF).astype(F32)
        tabs[8 + t] = top
        tabs[12] = top
        return carry

    lax.fori_loop(0, panels, forward, 0)

    nothing = jnp.zeros((GROUP, chips * 128), BF)
    fix = dot(nothing, tops[3], NT).astype(BF).astype(F32)
    top = (tabs[12] + fix).astype(BF).astype(F32)
    tabs[12] = top
    send_field(jnp.int32(3), top)

    def backward(t, carry):
        p = 6 - t
        value = (tabs[5 + p] * tabs[12]).astype(BF)

        def meanwhile():
            wait_sends(t - 1, lax.rem(t + 1, 2))

            @pl.when(t < chunks)
            def _():
                lifts(t)

        fixed = solve(t, p, value, meanwhile).astype(BF).astype(F32)
        top = (tabs[8 + p] + fixed).astype(BF).astype(F32)
        tabs[12] = top
        send_field(p, top)
        return carry

    lax.fori_loop(4, STEPS, backward, 0)
    wait_sends(STEPS - 1, (STEPS - 1) % 2)
    crossed = [first_right, first_left, second_right, second_left, on_right, on_left]
    for copy in scale_sends + piece_sends + crossed + shares:
        copy.wait_send()

    for k in range(8):
        @pl.when(k != r * 2 + c)
        def _():
            remote(field.at[0], own_w.at[k], o_send.at[0, 0], o_recv.at[k, 0], dev(r, m, other)).wait_recv()

        remote(field.at[0], nb_w.at[k], o_send.at[0, 0], o_recv.at[k, 1], dev(r, m, other)).wait_recv()
    for p in range(panels):
        @pl.when(p != r)
        def _():
            remote(field.at[p], own_w.at[0], o_send.at[p, 0], o_recv.at[0, 0], dev(r, m, other)).wait_send()

        for copy in field_copies(p):
            copy.wait_send()

    own = own_w[...].reshape(128, 128)
    window = jnp.concatenate([own, nb_w[...].reshape(128, 128)], axis=1)
    turned = jnp.transpose(own.astype(F32))
    half[...] = jnp.where(c == 0, turned[:64], turned[64:]).astype(BF)
    top_out = pltpu.make_async_copy(half, tf_hbm.at[0], out_sem.at[chunks])
    top_out.start()
    outs = []
    for g in range(chunks):
        cols = slice(g * per * width, (g + 1) * per * width)
        vec[:, cols] = (inner[:, cols].astype(F32) - dot(window, lift[:, cols], NN)).astype(BF)
        outs.append(pltpu.make_async_copy(vec.at[:, cols], lf_hbm.at[0, :, cols], out_sem.at[g]))
        outs[-1].start()
    for copy in outs:
        copy.wait()
    top_out.wait()


def body(sizes, top_source, leaf_source, top_inverse, leaf_inverse, boundary, touch_rows, coupling):
    ny, nz, chunks, per = sizes
    leaves, width = leaf_inverse.shape[1:3]
    reach = boundary.shape[2]
    columns = leaves * width
    order = ny * nz * 128
    any_spec = pl.BlockSpec(memory_space=pl.ANY)
    hbm_spec = pl.BlockSpec(memory_space=pltpu.HBM)
    dma = pltpu.SemaphoreType.DMA
    vmem = pltpu.VMEM
    operands = [
        pltpu.with_memory_space_constraint(x, pltpu.HBM)
        for x in (
            jnp.swapaxes(top_source, 1, 2), leaf_source, top_inverse, leaf_inverse, boundary,
            jnp.swapaxes(touch_rows, 0, 1), coupling,
        )
    ]
    top, leaf = pl.pallas_call(
        functools.partial(kernel, sizes),
        out_shape=(
            jax.ShapeDtypeStruct((1, 64, 128), BF),
            jax.ShapeDtypeStruct(leaf_source.shape, BF),
        ),
        in_specs=[hbm_spec] * 7,
        out_specs=(any_spec, any_spec),
        scratch_shapes=[
            vmem((64, 128), BF),
            vmem((128, columns), BF),
            vmem((leaves, width, width), BF),
            vmem((leaves, reach, width), BF),
            vmem((leaves, 1, reach), jnp.int32),
            vmem((1, 64), F32),
            vmem((128, columns), BF),
            vmem((256, columns), BF),
            vmem((128, 256), F32),
            vmem((8, GROUP, 128), BF),
            vmem((8, GROUP, 128), BF),
            vmem((4, 2, GROUP, 128), BF),
            vmem((4, 2, GROUP, 128), BF),
            vmem((8, 128), F32),
            vmem((4, 2, 8, 128), F32),
            vmem((4, 128, order), BF),
            vmem((STEPS, ny * nz, GROUP, 128), BF),
            vmem((16, GROUP, 128), F32),
            vmem((4, GROUP, 128), BF),
            vmem((8, GROUP, 128), BF),
            vmem((8, GROUP, 128), BF),
            vmem((64, 128), BF),
            dma((3, chunks)), dma((4,)), dma((chunks + 1,)),
            dma((6,)), dma((6,)), dma((7,)), dma((7,)),
            dma((8,)), dma((4, 2)), dma((8,)), dma((4, 2)), dma((8,)), dma((4, 2)),
            dma((2, ny * nz - 1)), dma((2, ny * nz)),
            dma((4, 4)), dma((8, 2)),
        ],
        compiler_params=pltpu.CompilerParams(
            collective_id=0, has_side_effects=True, vmem_limit_bytes=50 * 1024 * 1024
        ),
    )(*operands)
    return jnp.swapaxes(top, 1, 2), leaf


def solution(mesh, sizes=(4, 8, 6, 6)):
    placed = (
        P("panel", None, "front"),
        P("panel", None, "front"),
        P("panel", "front", None),
        P("panel", "front", None, None),
        P("panel", "front", None, None),
        P("panel", "front", None),
        P("panel", "front"),
    )
    return jax.shard_map(
        functools.partial(body, sizes),
        mesh=mesh,
        in_specs=placed,
        out_specs=(P("panel", None, "front"), P("panel", None, "front")),
        check_vma=False,
    )
```

```python
import functools

import jax
import jax.numpy as jnp
from jax import lax
from jax.experimental import pallas as pl
from jax.experimental.pallas import tpu as pltpu
from jax.sharding import PartitionSpec as P

MESH = pl.DeviceIdType.MESH
BF = jnp.bfloat16
F32 = jnp.float32
NT = (((1,), (1,)), ((), ()))
NN = (((1,), (0,)), ((), ()))
STEPS = 7
GROUP = 16


def dot(a, b, dims):
    return lax.dot_general(a, b, dims, preferred_element_type=F32)


def kernel(
    sizes,
    ts_hbm, ls_hbm, ti_hbm, li_hbm, bd_hbm, tr_hbm, cp_hbm,
    tf_out, lf_out,
    ts, vec, inv, bnd, rows, cpl,
    inner, lift, acc, main, halo, main_in, halo_in, scale, scale_in, tops, gath, tabs, field, own_w, nb_w,
    in_sem, small_sem,
    ta_send, ta_recv, tc_send, tc_recv,
    pm_send, pm_recv, ph_send, ph_recv, pc_send, pc_recv,
    g_send, g_recv, o_send, o_recv,
):
    ny, nz, chunks, per = sizes
    chips = ny * nz
    panels = 4
    r = lax.axis_index("panel")
    f = lax.axis_index("front")
    m, c = lax.div(f, 2), lax.rem(f, 2)
    y, z = lax.div(m, nz), lax.rem(m, nz)
    other = 1 - c
    up, down = lax.rem(m + 1, chips), lax.rem(m + chips - 1, chips)
    side = lax.rem(m + chips - 1 + 2 * c, chips)

    def dev(q, chip, core):
        return (q, chip * 2 + core)

    def chip_at(dy, dz):
        return lax.rem(y + dy, ny) * nz + lax.rem(z + dz, nz)

    steps_away = sorted(
        ((dy, dz) for dy in range(ny) for dz in range(nz) if dy or dz),
        key=lambda d: -min(d[0], ny - d[0]) - min(d[1], nz - d[1]),
    )

    def remote(src, dst, send, recv, where):
        return pltpu.make_async_remote_copy(
            src_ref=src, dst_ref=dst, send_sem=send, recv_sem=recv,
            device_id=where, device_id_type=MESH,
        )

    width = ls_hbm.shape[2] // chunks // per

    small = [
        pltpu.make_async_copy(ts_hbm.at[0], ts, small_sem.at[0]),
        pltpu.make_async_copy(tr_hbm, rows, small_sem.at[1]),
        pltpu.make_async_copy(cp_hbm, cpl, small_sem.at[2]),
        pltpu.make_async_copy(
            ti_hbm.at[0], tops.at[r, pl.ds(pl.multiple_of(c * 64, 64), 64)], small_sem.at[3]
        ),
    ]

    def big(g):
        at = pl.ds(g * per, per)
        cols = pl.ds(pl.multiple_of(g * (per * width), per * width), per * width)
        return (
            pltpu.make_async_copy(ls_hbm.at[0, :, cols], vec.at[:, cols], in_sem.at[2, g]),
            pltpu.make_async_copy(li_hbm.at[0, at], inv.at[at], in_sem.at[1, g]),
            pltpu.make_async_copy(bd_hbm.at[0, at], bnd.at[at], in_sem.at[0, g]),
        )

    small[1].start()
    for copy in big(0):
        copy.start()
    for copy in (small[0], small[2], small[3]):
        copy.start()
    for g in range(1, chunks):
        for copy in big(g):
            copy.start()

    barrier = pltpu.get_barrier_semaphore()
    peers = [dev(r, chip_at(dy, dz), c) for dy, dz in steps_away]
    beyond = lax.rem(m + chips + 1 - 2 * c, chips)
    for dq in range(panels):
        q = lax.rem(r + dq, panels)
        if dq:
            peers += [dev(q, m, c), dev(q, side, c), dev(q, beyond, c)]
        peers += [dev(q, m, other), dev(q, side, other)]
    for peer in peers:
        pl.semaphore_signal(barrier, inc=1, device_id=peer, device_id_type=MESH)

    acc[...] = jnp.zeros_like(acc)
    base = m * 128
    small[1].wait()

    def columns_of(j):
        return pl.ds(pl.multiple_of(j * width, width), width)

    def hot_rows(j):
        u = jnp.bitwise_and(rows[j] - base, 255)
        hot = lax.broadcasted_iota(jnp.int32, (256, u.shape[1]), 0) == u
        return jnp.where(hot, 1.0, 0.0).astype(BF)

    def leaf(j):
        solved = dot(vec[:, columns_of(j)], inv[j], NT).astype(BF)
        inner[:, columns_of(j)] = solved
        return dot(solved, bnd[j], NT).astype(BF)

    def leaves(g, carry):
        for copy in big(g):
            copy.wait()
        first = g * per
        pushed = jnp.concatenate([leaf(first + i) for i in range(per)], axis=1)
        hot = jnp.concatenate([hot_rows(first + i) for i in range(per)], axis=1)
        acc[...] += dot(pushed, hot, NT)
        return carry

    def lifts(g):
        for i in range(per):
            j = g * per + i
            spread = dot(hot_rows(j), bnd[j], NN).astype(BF)
            lift[:, columns_of(j)] = dot(spread, inv[j], NT).astype(BF)

    early = 1
    lax.fori_loop(0, early, leaves, 0)
    pl.semaphore_wait(barrier, len(peers))

    right, left, far = lax.rem(r + 1, 4), lax.rem(r + 3, 4), lax.rem(r + 2, 4)

    def rows_of(q, core, start=0, size=32):
        return tops.at[q, pl.ds(pl.multiple_of(core * 64 + start, 32), size)]

    def across(n, q, start, to, fresh):
        dst = rows_of(q, c, start)
        src = ti_hbm.at[0, pl.ds(start, 32)] if fresh else dst
        return remote(src, dst, ta_send.at[n], ta_recv.at[n], dev(to, m, c))

    def share(n, q, start, size=32):
        part = rows_of(q, c, start, size)
        src = ti_hbm.at[0] if size == 64 else part
        return remote(src, part, tc_send.at[n], tc_recv.at[n], dev(r, m, other))

    first_right, first_left = across(0, r, 0, right, True), across(1, r, 32, left, True)
    second_right, second_left = across(2, r, 32, right, True), across(3, r, 0, left, True)
    on_right, on_left = across(4, left, 0, right, False), across(5, right, 32, left, False)
    shares = [
        share(0, r, 0, 64), share(1, left, 0), share(2, right, 32), share(3, left, 32),
        share(4, right, 0), share(5, far, 0), share(6, far, 32),
    ]
    small[2].wait()
    own_scale = cpl[...]
    blank = jnp.zeros_like(own_scale)
    own_scale = jnp.concatenate(
        [jnp.where(c == 0, own_scale, blank), jnp.where(c == 0, blank, own_scale)], axis=1
    )
    scale[...] = jnp.broadcast_to(own_scale, scale.shape)
    scale_in[r, c] = scale[...]
    scale_sends = []
    for dq in range(panels):
        q = lax.rem(r + dq, panels)
        for n, core in enumerate((c, other)):
            if dq or n:
                scale_sends.append(remote(
                    scale, scale_in.at[r, c], pc_send.at[dq * 2 + n], pc_recv.at[r, c], dev(q, m, core)
                ))
    for copy in scale_sends:
        copy.start()
    first_right.start()
    first_left.start()
    shares[0].start()

    lax.fori_loop(early, chunks, leaves, 0)

    small[0].wait()
    known = -acc[:, :128]
    local = ts[...].astype(F32)
    zero = jnp.zeros_like(local)
    lower = jnp.where(c == 0, local, zero)
    upper = jnp.where(c == 0, zero, local)
    known = known + jnp.transpose(jnp.concatenate([lower, upper], axis=0))
    for k in range(8):
        main[k] = known[k * GROUP : (k + 1) * GROUP].astype(BF)
        halo[k] = (-acc[k * GROUP : (k + 1) * GROUP, 128:]).astype(BF)
    mine = r * 2 + c
    main_in[r, c] = main[mine]

    piece_sends = []
    for dq in range(panels):
        q = lax.rem(r + dq, panels)
        for n, core in enumerate((c, other)):
            k, slot = q * 2 + core, dq * 2 + n
            if slot:
                piece_sends.append(remote(
                    main.at[k], main_in.at[r, c], pm_send.at[slot], pm_recv.at[r, c], dev(q, m, core)
                ))
            piece_sends.append(remote(
                halo.at[k], halo_in.at[r, c], ph_send.at[slot], ph_recv.at[r, c], dev(q, side, core)
            ))
    for copy in piece_sends:
        copy.start()

    @pl.when(r == 0)
    def _():
        second_right.start()

    @pl.when(r < 3)
    def _():
        second_left.start()

    first_right.wait_recv()
    on_right.start()
    shares[1].start()
    first_left.wait_recv()
    on_left.start()
    shares[2].start()

    @pl.when(r > 0)
    def _():
        second_right.start()

    @pl.when(r == 3)
    def _():
        second_left.start()

    def meet_tops(t):
        away = lax.rem(t + panels - r, panels)

        @pl.when(away == 0)
        def _():
            small[3].wait()
            shares[0].wait_recv()

        @pl.when(away == 1)
        def _():
            second_left.wait_recv()
            shares[4].start()
            shares[2].wait_recv()
            shares[4].wait_recv()

        @pl.when(away == 2)
        def _():
            on_right.wait_recv()
            shares[5].start()
            on_left.wait_recv()
            shares[6].start()
            shares[5].wait_recv()
            shares[6].wait_recv()

        @pl.when(away == 3)
        def _():
            second_right.wait_recv()
            shares[3].start()
            shares[1].wait_recv()
            shares[3].wait_recv()

    def meet_pieces(p):
        for core in (0, 1):
            for_main = remote(main.at[0], main_in.at[p, core], pm_send.at[0], pm_recv.at[p, core], dev(r, m, other))
            for_scale = remote(scale, scale_in.at[p, core], pc_send.at[0], pc_recv.at[p, core], dev(r, m, other))

            @pl.when(jnp.logical_or(p != r, c != core))
            def _():
                for_scale.wait_recv()
                for_main.wait_recv()

            remote(halo.at[0], halo_in.at[p, core], ph_send.at[0], ph_recv.at[p, core], dev(r, m, other)).wait_recv()
        terms = [ref[p, core].astype(F32) for ref in (main_in, halo_in) for core in (0, 1)]
        tabs[p] = (terms[0] + terms[1]) + (terms[2] + terms[3])
        pair = scale_in[p, 0] + scale_in[p, 1]
        tabs[4 + p] = jnp.concatenate([pair, pair], axis=0)

    def sends(t, s):
        return [
            remote(gath.at[t, m], gath.at[t, m], g_send.at[s, n], g_recv.at[s, m], dev(r, chip_at(dy, dz), c))
            for n, (dy, dz) in enumerate(steps_away)
        ]

    def wait_sends(t, s):
        for copy in sends(t, s):
            copy.wait_send()

    def arrived(t, s, tile):
        remote(gath.at[t, tile], gath.at[t, tile], g_send.at[s, 0], g_recv.at[s, tile], dev(r, m, other)).wait_recv()

    def solve(t, p, value, meanwhile):
        s = lax.rem(t, 2)
        gath[t, m] = value
        for copy in sends(t, s):
            copy.start()
        meanwhile()
        total = jnp.zeros((GROUP, 128), F32)
        nearest = [(0, 0)] + steps_away[::-1]
        cuts = sorted({0} | {len(nearest) * k // 16 for k in (4, 8, 12, 15, 16)})
        for low, high in zip(cuts, cuts[1:]):
            tiles = [chip_at(dy, dz) for dy, dz in nearest[low:high]]
            for n, tile in enumerate(tiles):
                if low + n:
                    arrived(t, s, tile)
            x = jnp.concatenate([gath[t, tile] for tile in tiles], axis=1)
            w = [tops[p, :, pl.ds(pl.multiple_of(tile * 128, 128), 128)] for tile in tiles]
            total += dot(x, jnp.concatenate(w, axis=1), NT)
        return total

    def send_field(p, value):
        field[p] = value.astype(BF)
        mine = r * 2 + c

        @pl.when(p == r)
        def _():
            own_w[mine] = value.astype(BF)

        @pl.when(p != r)
        def _():
            remote(field.at[p], own_w.at[mine], o_send.at[p, 0], o_recv.at[mine, 0], dev(p, m, c)).start()

        for copy in field_copies(p):
            copy.start()

    def field_copies(p):
        mine = r * 2 + c
        return [
            remote(field.at[p], own_w.at[mine], o_send.at[p, 1], o_recv.at[mine, 0], dev(p, m, other)),
            remote(field.at[p], nb_w.at[mine], o_send.at[p, 2], o_recv.at[mine, 1], dev(p, down, 1)),
            remote(field.at[p], nb_w.at[mine], o_send.at[p, 3], o_recv.at[mine, 1], dev(p, up, 0)),
        ]

    tabs[12] = jnp.zeros((GROUP, 128), F32)

    def forward(t, carry):
        meet_pieces(t)
        value = (tabs[t] + tabs[4 + t] * tabs[12]).astype(BF)

        def meanwhile():
            @pl.when(t > 0)
            def _():
                wait_sends(t - 1, lax.rem(t + 1, 2))

            lifts(t)
            meet_tops(t)

        top = solve(t, t, value, meanwhile).astype(BF).astype(F32)
        tabs[8 + t] = top
        tabs[12] = top
        return carry

    lax.fori_loop(0, panels, forward, 0)

    nothing = jnp.zeros((GROUP, chips * 128), BF)
    fix = dot(nothing, tops[3], NT).astype(BF).astype(F32)
    top = (tabs[12] + fix).astype(BF).astype(F32)
    tabs[12] = top
    send_field(jnp.int32(3), top)

    def backward(t, carry):
        p = 6 - t
        value = (tabs[5 + p] * tabs[12]).astype(BF)

        def meanwhile():
            wait_sends(t - 1, lax.rem(t + 1, 2))

            @pl.when(t < chunks)
            def _():
                lifts(t)

        fixed = solve(t, p, value, meanwhile).astype(BF).astype(F32)
        top = (tabs[8 + p] + fixed).astype(BF).astype(F32)
        tabs[12] = top
        send_field(p, top)
        return carry

    lax.fori_loop(4, STEPS, backward, 0)
    wait_sends(STEPS - 1, (STEPS - 1) % 2)
    crossed = [first_right, first_left, second_right, second_left, on_right, on_left]
    for copy in scale_sends + piece_sends + crossed + shares:
        copy.wait_send()

    for k in range(8):
        @pl.when(k != r * 2 + c)
        def _():
            remote(field.at[0], own_w.at[k], o_send.at[0, 0], o_recv.at[k, 0], dev(r, m, other)).wait_recv()

        remote(field.at[0], nb_w.at[k], o_send.at[0, 0], o_recv.at[k, 1], dev(r, m, other)).wait_recv()
    for p in range(panels):
        @pl.when(p != r)
        def _():
            remote(field.at[p], own_w.at[0], o_send.at[p, 0], o_recv.at[0, 0], dev(r, m, other)).wait_send()

        for copy in field_copies(p):
            copy.wait_send()

    own = own_w[...].reshape(128, 128)
    window = jnp.concatenate([own, nb_w[...].reshape(128, 128)], axis=1)
    turned = jnp.transpose(own.astype(F32))
    tf_out[0] = jnp.where(c == 0, turned[:64], turned[64:]).astype(BF)
    for g in range(chunks):
        cols = slice(g * per * width, (g + 1) * per * width)
        lf_out[0, :, cols] = (inner[:, cols].astype(F32) - dot(window, lift[:, cols], NN)).astype(BF)


def body(sizes, top_source, leaf_source, top_inverse, leaf_inverse, boundary, touch_rows, coupling):
    ny, nz, chunks, per = sizes
    leaves, width = leaf_inverse.shape[1:3]
    reach = boundary.shape[2]
    columns = leaves * width
    order = ny * nz * 128
    hbm_spec = pl.BlockSpec(memory_space=pltpu.HBM)
    dma = pltpu.SemaphoreType.DMA
    vmem = pltpu.VMEM
    operands = [
        pltpu.with_memory_space_constraint(x, pltpu.HBM)
        for x in (
            jnp.swapaxes(top_source, 1, 2), leaf_source, top_inverse, leaf_inverse, boundary,
            jnp.swapaxes(touch_rows, 0, 1), coupling,
        )
    ]
    top, leaf = pl.pallas_call(
        functools.partial(kernel, sizes),
        out_shape=(
            jax.ShapeDtypeStruct((1, 64, 128), BF),
            jax.ShapeDtypeStruct(leaf_source.shape, BF),
        ),
        in_specs=[hbm_spec] * 7,
        out_specs=(pl.BlockSpec(memory_space=pltpu.VMEM),) * 2,
        scratch_shapes=[
            vmem((64, 128), BF),
            vmem((128, columns), BF),
            vmem((leaves, width, width), BF),
            vmem((leaves, reach, width), BF),
            vmem((leaves, 1, reach), jnp.int32),
            vmem((1, 64), F32),
            vmem((128, columns), BF),
            vmem((256, columns), BF),
            vmem((128, 256), F32),
            vmem((8, GROUP, 128), BF),
            vmem((8, GROUP, 128), BF),
            vmem((4, 2, GROUP, 128), BF),
            vmem((4, 2, GROUP, 128), BF),
            vmem((8, 128), F32),
            vmem((4, 2, 8, 128), F32),
            vmem((4, 128, order), BF),
            vmem((STEPS, ny * nz, GROUP, 128), BF),
            vmem((16, GROUP, 128), F32),
            vmem((4, GROUP, 128), BF),
            vmem((8, GROUP, 128), BF),
            vmem((8, GROUP, 128), BF),
            dma((3, chunks)), dma((4,)),
            dma((6,)), dma((6,)), dma((7,)), dma((7,)),
            dma((8,)), dma((4, 2)), dma((8,)), dma((4, 2)), dma((8,)), dma((4, 2)),
            dma((2, ny * nz - 1)), dma((2, ny * nz)),
            dma((4, 4)), dma((8, 2)),
        ],
        compiler_params=pltpu.CompilerParams(
            collective_id=0, has_side_effects=True, vmem_limit_bytes=50 * 1024 * 1024
        ),
    )(*operands)
    return jnp.swapaxes(top, 1, 2), leaf


def solution(mesh, sizes=(4, 8, 6, 6)):
    placed = (
        P("panel", None, "front"),
        P("panel", None, "front"),
        P("panel", "front", None),
        P("panel", "front", None, None),
        P("panel", "front", None, None),
        P("panel", "front", None),
        P("panel", "front"),
    )
    return jax.shard_map(
        functools.partial(body, sizes),
        mesh=mesh,
        in_specs=placed,
        out_specs=(P("panel", None, "front"), P("panel", None, "front")),
        check_vma=False,
    )
```

```python
import functools

import jax
import jax.numpy as jnp
from jax import lax
from jax.experimental import pallas as pl
from jax.experimental.pallas import tpu as pltpu
from jax.sharding import PartitionSpec as P

MESH = pl.DeviceIdType.MESH
BF = jnp.bfloat16
F32 = jnp.float32
NT = (((1,), (1,)), ((), ()))
NN = (((1,), (0,)), ((), ()))
STEPS = 7
GROUP = 16


def dot(a, b, dims):
    return lax.dot_general(a, b, dims, preferred_element_type=F32)


def kernel(
    sizes,
    ts_hbm, ls_hbm, ti_hbm, li_hbm, bd_hbm, tr_hbm, cp_hbm,
    tf_out, lf_out,
    ts, vec, inv, bnd, rows, cpl,
    inner, lift, acc, main, halo, main_in, halo_in, scale, scale_in, tops, gath, tabs, field, own_w, nb_w,
    in_sem, small_sem,
    ta_send, ta_recv, tc_send, tc_recv,
    pm_send, pm_recv, ph_send, ph_recv, pc_send, pc_recv,
    g_send, g_recv, o_send, o_recv,
):
    ny, nz, chunks, per = sizes
    chips = ny * nz
    panels = 4
    r = lax.axis_index("panel")
    f = lax.axis_index("front")
    m, c = lax.div(f, 2), lax.rem(f, 2)
    y, z = lax.div(m, nz), lax.rem(m, nz)
    other = 1 - c
    up, down = lax.rem(m + 1, chips), lax.rem(m + chips - 1, chips)
    side = lax.rem(m + chips - 1 + 2 * c, chips)

    def dev(q, chip, core):
        return (q, chip * 2 + core)

    def chip_at(dy, dz):
        return lax.rem(y + dy, ny) * nz + lax.rem(z + dz, nz)

    steps_away = sorted(
        ((dy, dz) for dy in range(ny) for dz in range(nz) if dy or dz),
        key=lambda d: -min(d[0], ny - d[0]) - min(d[1], nz - d[1]),
    )

    def remote(src, dst, send, recv, where):
        return pltpu.make_async_remote_copy(
            src_ref=src, dst_ref=dst, send_sem=send, recv_sem=recv,
            device_id=where, device_id_type=MESH,
        )

    width = ls_hbm.shape[2] // chunks // per

    small = [
        pltpu.make_async_copy(ts_hbm.at[0], ts, small_sem.at[0]),
        pltpu.make_async_copy(tr_hbm, rows, small_sem.at[1]),
        pltpu.make_async_copy(cp_hbm, cpl, small_sem.at[2]),
        pltpu.make_async_copy(
            ti_hbm.at[0], tops.at[r, pl.ds(pl.multiple_of(c * 64, 64), 64)], small_sem.at[3]
        ),
    ]

    def big(g):
        at = pl.ds(g * per, per)
        cols = pl.ds(pl.multiple_of(g * (per * width), per * width), per * width)
        return (
            pltpu.make_async_copy(ls_hbm.at[0, :, cols], vec.at[:, cols], in_sem.at[2, g]),
            pltpu.make_async_copy(li_hbm.at[0, at], inv.at[at], in_sem.at[1, g]),
            pltpu.make_async_copy(bd_hbm.at[0, at], bnd.at[at], in_sem.at[0, g]),
        )

    small[1].start()
    for copy in big(0):
        copy.start()
    for copy in (small[0], small[2], small[3]):
        copy.start()
    for g in range(1, chunks):
        for copy in big(g):
            copy.start()

    barrier = pltpu.get_barrier_semaphore()
    peers = [dev(r, chip_at(dy, dz), c) for dy, dz in steps_away]
    beyond = lax.rem(m + chips + 1 - 2 * c, chips)
    for dq in range(panels):
        q = lax.rem(r + dq, panels)
        if dq:
            peers += [dev(q, m, c), dev(q, side, c), dev(q, beyond, c)]
        peers += [dev(q, m, other), dev(q, side, other)]
    for peer in peers:
        pl.semaphore_signal(barrier, inc=1, device_id=peer, device_id_type=MESH)

    acc[...] = jnp.zeros_like(acc)
    base = m * 128
    small[1].wait()

    def columns_of(j):
        return pl.ds(pl.multiple_of(j * width, width), width)

    def hot_rows(j):
        u = jnp.bitwise_and(rows[j] - base, 255)
        hot = lax.broadcasted_iota(jnp.int32, (256, u.shape[1]), 0) == u
        return jnp.where(hot, 1.0, 0.0).astype(BF)

    def leaf(j):
        solved = dot(vec[:, columns_of(j)], inv[j], NT).astype(BF)
        inner[:, columns_of(j)] = solved
        return dot(solved, bnd[j], NT).astype(BF)

    def leaves(g, carry):
        for copy in big(g):
            copy.wait()
        first = g * per
        pushed = jnp.concatenate([leaf(first + i) for i in range(per)], axis=1)
        hot = jnp.concatenate([hot_rows(first + i) for i in range(per)], axis=1)
        acc[...] += dot(pushed, hot, NT)
        return carry

    def lifts(g):
        for i in range(per):
            j = g * per + i
            spread = dot(hot_rows(j), bnd[j], NN).astype(BF)
            lift[:, columns_of(j)] = dot(spread, inv[j], NT).astype(BF)

    early = 1
    lax.fori_loop(0, early, leaves, 0)
    pl.semaphore_wait(barrier, len(peers))

    right, left, far = lax.rem(r + 1, 4), lax.rem(r + 3, 4), lax.rem(r + 2, 4)

    def rows_of(q, core, start=0, size=32):
        return tops.at[q, pl.ds(pl.multiple_of(core * 64 + start, 32), size)]

    def across(n, q, start, to, fresh):
        dst = rows_of(q, c, start)
        src = ti_hbm.at[0, pl.ds(start, 32)] if fresh else dst
        return remote(src, dst, ta_send.at[n], ta_recv.at[n], dev(to, m, c))

    def share(n, q, start, size=32):
        part = rows_of(q, c, start, size)
        src = ti_hbm.at[0] if size == 64 else part
        return remote(src, part, tc_send.at[n], tc_recv.at[n], dev(r, m, other))

    first_right, first_left = across(0, r, 0, right, True), across(1, r, 32, left, True)
    second_right, second_left = across(2, r, 32, right, True), across(3, r, 0, left, True)
    on_right, on_left = across(4, left, 0, right, False), across(5, right, 32, left, False)
    shares = [
        share(0, r, 0, 64), share(1, left, 0), share(2, right, 32), share(3, left, 32),
        share(4, right, 0), share(5, far, 0), share(6, far, 32),
    ]
    small[2].wait()
    own_scale = cpl[...]
    blank = jnp.zeros_like(own_scale)
    own_scale = jnp.concatenate(
        [jnp.where(c == 0, own_scale, blank), jnp.where(c == 0, blank, own_scale)], axis=1
    )
    scale[...] = jnp.broadcast_to(own_scale, scale.shape)
    scale_in[r, c] = scale[...]
    scale_sends = []
    for dq in range(panels):
        q = lax.rem(r + dq, panels)
        for n, core in enumerate((c, other)):
            if dq or n:
                scale_sends.append(remote(
                    scale, scale_in.at[r, c], pc_send.at[dq * 2 + n], pc_recv.at[r, c], dev(q, m, core)
                ))
    for copy in scale_sends:
        copy.start()
    first_right.start()
    first_left.start()
    shares[0].start()

    lax.fori_loop(early, chunks, leaves, 0)

    small[0].wait()
    known = -acc[:, :128]
    local = ts[...].astype(F32)
    zero = jnp.zeros_like(local)
    lower = jnp.where(c == 0, local, zero)
    upper = jnp.where(c == 0, zero, local)
    known = known + jnp.transpose(jnp.concatenate([lower, upper], axis=0))
    for k in range(8):
        main[k] = known[k * GROUP : (k + 1) * GROUP].astype(BF)
        halo[k] = (-acc[k * GROUP : (k + 1) * GROUP, 128:]).astype(BF)
    mine = r * 2 + c
    main_in[r, c] = main[mine]

    piece_sends = []
    for dq in (2, 1, 3, 0):
        q = lax.rem(r + dq, panels)
        for n, core in enumerate((c, other)):
            k, slot = q * 2 + core, dq * 2 + n
            piece_sends.append(remote(
                halo.at[k], halo_in.at[r, c], ph_send.at[slot], ph_recv.at[r, c], dev(q, side, core)
            ))
            if slot:
                piece_sends.append(remote(
                    main.at[k], main_in.at[r, c], pm_send.at[slot], pm_recv.at[r, c], dev(q, m, core)
                ))
    for copy in piece_sends:
        copy.start()

    @pl.when(r == 0)
    def _():
        second_right.start()

    @pl.when(r < 3)
    def _():
        second_left.start()

    first_right.wait_recv()
    on_right.start()
    shares[1].start()
    first_left.wait_recv()
    on_left.start()
    shares[2].start()

    @pl.when(r > 0)
    def _():
        second_right.start()

    @pl.when(r == 3)
    def _():
        second_left.start()

    def meet_tops(t):
        away = lax.rem(t + panels - r, panels)

        @pl.when(away == 0)
        def _():
            small[3].wait()
            shares[0].wait_recv()

        @pl.when(away == 1)
        def _():
            second_left.wait_recv()
            shares[4].start()
            shares[2].wait_recv()
            shares[4].wait_recv()

        @pl.when(away == 2)
        def _():
            on_right.wait_recv()
            shares[5].start()
            on_left.wait_recv()
            shares[6].start()
            shares[5].wait_recv()
            shares[6].wait_recv()

        @pl.when(away == 3)
        def _():
            second_right.wait_recv()
            shares[3].start()
            shares[1].wait_recv()
            shares[3].wait_recv()

    def meet_pieces(p):
        for core in (0, 1):
            for_main = remote(main.at[0], main_in.at[p, core], pm_send.at[0], pm_recv.at[p, core], dev(r, m, other))
            for_scale = remote(scale, scale_in.at[p, core], pc_send.at[0], pc_recv.at[p, core], dev(r, m, other))

            @pl.when(jnp.logical_or(p != r, c != core))
            def _():
                for_scale.wait_recv()
                for_main.wait_recv()

            remote(halo.at[0], halo_in.at[p, core], ph_send.at[0], ph_recv.at[p, core], dev(r, m, other)).wait_recv()
        terms = [ref[p, core].astype(F32) for ref in (main_in, halo_in) for core in (0, 1)]
        tabs[p] = (terms[0] + terms[1]) + (terms[2] + terms[3])
        pair = scale_in[p, 0] + scale_in[p, 1]
        tabs[4 + p] = jnp.concatenate([pair, pair], axis=0)

    def sends(t, s):
        return [
            remote(gath.at[t, m], gath.at[t, m], g_send.at[s, n], g_recv.at[s, m], dev(r, chip_at(dy, dz), c))
            for n, (dy, dz) in enumerate(steps_away)
        ]

    def wait_sends(t, s):
        for copy in sends(t, s):
            copy.wait_send()

    def arrived(t, s, tile):
        remote(gath.at[t, tile], gath.at[t, tile], g_send.at[s, 0], g_recv.at[s, tile], dev(r, m, other)).wait_recv()

    def solve(t, p, value, meanwhile):
        s = lax.rem(t, 2)
        gath[t, m] = value
        for copy in sends(t, s):
            copy.start()
        meanwhile()
        total = jnp.zeros((GROUP, 128), F32)
        nearest = [(0, 0)] + steps_away[::-1]
        cuts = sorted({0} | {len(nearest) * k // 16 for k in (4, 8, 12, 15, 16)})
        for low, high in zip(cuts, cuts[1:]):
            tiles = [chip_at(dy, dz) for dy, dz in nearest[low:high]]
            for n, tile in enumerate(tiles):
                if low + n:
                    arrived(t, s, tile)
            x = jnp.concatenate([gath[t, tile] for tile in tiles], axis=1)
            w = [tops[p, :, pl.ds(pl.multiple_of(tile * 128, 128), 128)] for tile in tiles]
            total += dot(x, jnp.concatenate(w, axis=1), NT)
        return total

    def send_field(p, value):
        field[p] = value.astype(BF)
        mine = r * 2 + c

        @pl.when(p == r)
        def _():
            own_w[mine] = value.astype(BF)

        @pl.when(p != r)
        def _():
            remote(field.at[p], own_w.at[mine], o_send.at[p, 0], o_recv.at[mine, 0], dev(p, m, c)).start()

        for copy in field_copies(p):
            copy.start()

    def field_copies(p):
        mine = r * 2 + c
        return [
            remote(field.at[p], nb_w.at[mine], o_send.at[p, 2], o_recv.at[mine, 1], dev(p, down, 1)),
            remote(field.at[p], nb_w.at[mine], o_send.at[p, 3], o_recv.at[mine, 1], dev(p, up, 0)),
            remote(field.at[p], own_w.at[mine], o_send.at[p, 1], o_recv.at[mine, 0], dev(p, m, other)),
        ]

    tabs[12] = jnp.zeros((GROUP, 128), F32)

    def forward(t, carry):
        value = (tabs[t] + tabs[4 + t] * tabs[12]).astype(BF)

        def meanwhile():
            @pl.when(t > 0)
            def _():
                wait_sends(t - 1, lax.rem(t + 1, 2))

            lifts(t)
            meet_tops(t)

            @pl.when(t < panels - 1)
            def _():
                meet_pieces(t + 1)

        top = solve(t, t, value, meanwhile).astype(BF).astype(F32)
        tabs[8 + t] = top
        tabs[12] = top
        return carry

    meet_pieces(0)
    lax.fori_loop(0, panels, forward, 0)

    nothing = jnp.zeros((GROUP, chips * 128), BF)
    fix = dot(nothing, tops[3], NT).astype(BF).astype(F32)
    top = (tabs[12] + fix).astype(BF).astype(F32)
    tabs[12] = top
    send_field(jnp.int32(3), top)

    def backward(t, carry):
        p = 6 - t
        value = (tabs[5 + p] * tabs[12]).astype(BF)

        def meanwhile():
            wait_sends(t - 1, lax.rem(t + 1, 2))

            @pl.when(t < chunks)
            def _():
                lifts(t)

        fixed = solve(t, p, value, meanwhile).astype(BF).astype(F32)
        top = (tabs[8 + p] + fixed).astype(BF).astype(F32)
        tabs[12] = top
        send_field(p, top)
        return carry

    lax.fori_loop(4, STEPS, backward, 0)
    wait_sends(STEPS - 1, (STEPS - 1) % 2)
    crossed = [first_right, first_left, second_right, second_left, on_right, on_left]
    for copy in scale_sends + piece_sends + crossed + shares:
        copy.wait_send()

    for p in range(panels):
        @pl.when(p != r)
        def _():
            remote(field.at[p], own_w.at[0], o_send.at[p, 0], o_recv.at[0, 0], dev(r, m, other)).wait_send()

        for copy in field_copies(p):
            copy.wait_send()

    for k in range(8):
        @pl.when(k != r * 2 + c)
        def _():
            remote(field.at[0], own_w.at[k], o_send.at[0, 0], o_recv.at[k, 0], dev(r, m, other)).wait_recv()

        remote(field.at[0], nb_w.at[k], o_send.at[0, 0], o_recv.at[k, 1], dev(r, m, other)).wait_recv()
    own = own_w[...].reshape(128, 128)
    window = jnp.concatenate([own, nb_w[...].reshape(128, 128)], axis=1)
    turned = jnp.transpose(own.astype(F32))
    tf_out[0] = jnp.where(c == 0, turned[:64], turned[64:]).astype(BF)
    for g in range(chunks):
        cols = slice(g * per * width, (g + 1) * per * width)
        lf_out[0, :, cols] = (inner[:, cols].astype(F32) - dot(window, lift[:, cols], NN)).astype(BF)


def body(sizes, top_source, leaf_source, top_inverse, leaf_inverse, boundary, touch_rows, coupling):
    ny, nz, chunks, per = sizes
    leaves, width = leaf_inverse.shape[1:3]
    reach = boundary.shape[2]
    columns = leaves * width
    order = ny * nz * 128
    hbm_spec = pl.BlockSpec(memory_space=pltpu.HBM)
    dma = pltpu.SemaphoreType.DMA
    vmem = pltpu.VMEM
    operands = [
        pltpu.with_memory_space_constraint(x, pltpu.HBM)
        for x in (
            jnp.swapaxes(top_source, 1, 2), leaf_source, top_inverse, leaf_inverse, boundary,
            jnp.swapaxes(touch_rows, 0, 1), coupling,
        )
    ]
    top, leaf = pl.pallas_call(
        functools.partial(kernel, sizes),
        out_shape=(
            jax.ShapeDtypeStruct((1, 64, 128), BF),
            jax.ShapeDtypeStruct(leaf_source.shape, BF),
        ),
        in_specs=[hbm_spec] * 7,
        out_specs=(pl.BlockSpec(memory_space=pltpu.VMEM),) * 2,
        scratch_shapes=[
            vmem((64, 128), BF),
            vmem((128, columns), BF),
            vmem((leaves, width, width), BF),
            vmem((leaves, reach, width), BF),
            vmem((leaves, 1, reach), jnp.int32),
            vmem((1, 64), F32),
            vmem((128, columns), BF),
            vmem((256, columns), BF),
            vmem((128, 256), F32),
            vmem((8, GROUP, 128), BF),
            vmem((8, GROUP, 128), BF),
            vmem((4, 2, GROUP, 128), BF),
            vmem((4, 2, GROUP, 128), BF),
            vmem((8, 128), F32),
            vmem((4, 2, 8, 128), F32),
            vmem((4, 128, order), BF),
            vmem((STEPS, ny * nz, GROUP, 128), BF),
            vmem((16, GROUP, 128), F32),
            vmem((4, GROUP, 128), BF),
            vmem((8, GROUP, 128), BF),
            vmem((8, GROUP, 128), BF),
            dma((3, chunks)), dma((4,)),
            dma((6,)), dma((6,)), dma((7,)), dma((7,)),
            dma((8,)), dma((4, 2)), dma((8,)), dma((4, 2)), dma((8,)), dma((4, 2)),
            dma((2, ny * nz - 1)), dma((2, ny * nz)),
            dma((4, 4)), dma((8, 2)),
        ],
        compiler_params=pltpu.CompilerParams(
            collective_id=0, has_side_effects=True, vmem_limit_bytes=50 * 1024 * 1024
        ),
    )(*operands)
    return jnp.swapaxes(top, 1, 2), leaf


def solution(mesh, sizes=(4, 8, 6, 6)):
    placed = (
        P("panel", None, "front"),
        P("panel", None, "front"),
        P("panel", "front", None),
        P("panel", "front", None, None),
        P("panel", "front", None, None),
        P("panel", "front", None),
        P("panel", "front"),
    )
    return jax.shard_map(
        functools.partial(body, sizes),
        mesh=mesh,
        in_specs=placed,
        out_specs=(P("panel", None, "front"), P("panel", None, "front")),
        check_vma=False,
    )
```
